32 devices in a mesh: groups: 2 (over y), seq: 2 (over x), frame: 4 (over z), cfg: 2 (over core).
Axes of the slice: x: 2, y: 2, z: 4, core: 2. Of those that a mesh axis runs over, the one named last changes fastest.
Arguments:
- qkv: bfloat16 [2, 4096, 3, 4096], P('cfg', ('groups', 'frame', 'seq')), parts along dimension 1, may hold values from -108 to 108, as said below
- timestep: int32 [2], P('groups'), parts along dimension 0, may hold values from 0 to 999
- windows: int32 [32], replicated, may hold values from 0 to 2
- segments: int32 [16], P('groups'), parts along dimension 0, may hold values from 0 to 3, never falling along the last dimension, each value on 1 to 4 neighbouring positions
Outputs:
- guided: bfloat16 [4096, 16, 256], P(('groups', 'frame', 'seq'), 'cfg'), parts along dimension 0
The draws below stay inside these ranges and needn't reach their ends.
There are 2 independent parts, one for each index of `groups`. The reference program is written for one: setup_inputs(seed, part) draws one part's arguments, and reference() takes and returns one part's arrays. A program takes and returns all parts, laid end to end along the dimension named above; an argument that names none is the same for every part. Nothing has to cross between parts.
Inputs may be any that keep to these rules, and one draw needn't show every extreme that they name: Entries of qkv lie in this range. `segments`: shot numbers never fall from one frame to the next.
All inputs are finite; a program needn't handle non-finite values.
Results may differ from the reference program's by a relative error of at most 0.0053.
Values may be sent and summed in bfloat16 or wider, within the bound.
A program may use at most 128 MiB of HBM per device.

```python
import math
import jax
import jax.numpy as jnp
import numpy as np
from jax import lax

HD = 128
HEADS = 32
P_SIZE = 256
W_MAX = 2
SEGMENTS = 4
FRAMES = 8
TOKENS = 2048
N_SEQ = 2


def draw_qkv(key, part):
    key = jax.random.fold_in(key, 11)
    streams = jax.random.split(key, 1)
    shape = (2, TOKENS, 3, HEADS * HD)
    spreads = jnp.array([2.0, 1.0, 4.0], jnp.float32).reshape(1, 1, 3, 1)
    base = jnp.clip(jax.random.normal(streams[0], shape, jnp.float32), -5.0, 5.0)
    values = base * spreads
    return values.astype(jnp.bfloat16)


def draw_windows(key, part):
    key = jax.random.fold_in(key, 23)
    order = jax.random.permutation(key, HEADS)
    return (order % (W_MAX + 1)).astype(jnp.int32)


def length_profile(amount, total, most, slope):
    loads = [(1 << 20) // math.isqrt(rank ** slope) + 1 for rank in range(2, amount + 1)]
    spare, counts = total - most - (amount - 1), [1] * (amount - 1)
    while spare > 0:
        free = [i for i in range(amount - 1) if counts[i] < most]
        whole, left = sum([loads[i] for i in free]), spare
        for i in free:
            more = min(most - counts[i], max(1, left * loads[i] // whole), spare)
            counts[i] = counts[i] + more
            spare = spare - more
    return np.array([most] + counts)


def ragged(key, amount, total, most, slope):
    if amount == 2:
        one = jax.random.randint(key, (), max(1, total - most), min(most, total - 1) + 1)
        return jnp.stack([one, total - one])
    tallies = jnp.asarray(length_profile(amount, total, most, slope), jnp.int32)
    pairs = (amount - 1) // 2
    giver, taker = tallies[1:1 + 2 * pairs:2], tallies[2:2 + 2 * pairs:2]
    margin = jnp.minimum(giver - 1, most - taker)
    moved = jax.random.randint(jax.random.fold_in(key, 1), (pairs,), 0, 1 << 20) % (margin + 1)
    tallies = tallies.at[1:1 + 2 * pairs:2].set(giver - moved).at[2:2 + 2 * pairs:2].set(taker + moved)
    return tallies[jax.random.permutation(jax.random.fold_in(key, 2), amount)]


def setup_inputs(seed: int = 0, part: int = 0) -> dict:
    keys = jax.random.split(jax.random.key(seed), 5)
    own_keys = jax.random.split(jax.random.fold_in(keys[4], part), 5)
    qkv = draw_qkv(jax.random.fold_in(jax.random.fold_in(keys[4], part), 71), part)
    timestep = jax.random.randint(own_keys[1], (1,), 0, 1000).astype(jnp.int32)
    windows = draw_windows(jax.random.fold_in(keys[4], 71), part)
    segments = jnp.searchsorted(jnp.cumsum(ragged(own_keys[3], SEGMENTS, FRAMES, FRAMES // 2, 1)), jnp.arange(FRAMES), side="right").astype(jnp.int32)
    return {"qkv": qkv, "timestep": timestep, "windows": windows, "segments": segments}


def reference(qkv, timestep, windows, segments):
    scale = 1.0 / (HD ** 0.5)
    blocks = qkv.reshape(2, FRAMES, P_SIZE, 3, HEADS, HD)
    fill = jnp.full((W_MAX,), -1, jnp.int32)
    seg_pad = jnp.concatenate([fill, segments.astype(jnp.int32), fill])
    offsets = jnp.arange(2 * W_MAX + 1, dtype=jnp.int32) - W_MAX
    within_reach = jnp.abs(offsets)[None, :] <= windows.astype(jnp.int32)[:, None]

    def one_frame(frame_number):
        query = lax.dynamic_index_in_dim(blocks, frame_number, 1, keepdims=False)[:, :, 0]
        picks = jnp.clip(frame_number + offsets, 0, FRAMES - 1).astype(jnp.int32)
        near = jnp.take(blocks, picks, axis=1)
        key_rows = near[:, :, :, 1]
        value_rows = near[:, :, :, 2]
        shots = lax.dynamic_slice_in_dim(seg_pad, frame_number, 2 * W_MAX + 1, 0)
        own_shot = lax.dynamic_index_in_dim(seg_pad, frame_number + W_MAX, 0, keepdims=False)
        allowed = within_reach & (shots == own_shot)[None, :]
        scores = jnp.einsum('bthd,bgrhd->bhtgr', query.astype(jnp.float32), key_rows.astype(jnp.float32)) * scale
        scores = jnp.where(allowed[None, :, None, :, None], scores, -1e30)
        highest = jnp.max(scores, axis=(3, 4), keepdims=True)
        expd = jnp.exp(scores - highest)
        totals = jnp.sum(expd, axis=(3, 4))
        weights = expd.astype(jnp.bfloat16)
        mixed = jnp.einsum('bhtgr,bgrhd->bthd', weights.astype(jnp.float32), value_rows.astype(jnp.float32))
        mixed = mixed / jnp.transpose(totals, (0, 2, 1))[..., None]
        return mixed.astype(jnp.bfloat16)

    attended = lax.map(one_frame, jnp.arange(FRAMES, dtype=jnp.int32))
    strength = 1.0 + 4.0 * timestep[0].astype(jnp.float32) / 999.0
    cond = attended[:, 0].astype(jnp.float32)
    uncond = attended[:, 1].astype(jnp.float32)
    guided = (uncond + strength * (cond - uncond)).astype(jnp.bfloat16)
    guided = guided.reshape(TOKENS, N_SEQ, HEADS // N_SEQ, HD)
    guided = jnp.transpose(guided, (0, 2, 1, 3)).reshape(TOKENS, HEADS // N_SEQ, N_SEQ * HD)
    return guided
```

```python
import functools
import math

import jax
import jax.numpy as jnp
from jax import lax
from jax.experimental import pallas as pl
from jax.experimental.pallas import tpu as pltpu
from jax.sharding import PartitionSpec as P

HD = 128
W_MAX = 2
NEG = -1e30
LOG2E = 1.4426950408889634
MESH = pl.DeviceIdType.MESH


def kernel(
    dims, x_ref, time_ref, win_ref, seg_ref, out_ref,
    kv, qb, gb, kv_sem, q_sem, halo_sem, out_sem, a2a_send, own_send, relay_send, out_send,
):
    S, C, F, heads, tl, frames_here = dims
    rows = S * tl
    per_frame = rows // frames_here
    span = (2 * W_MAX + 1) * per_frame
    frames = F * frames_here
    s = lax.axis_index("seq")
    c = lax.axis_index("cfg")
    f = lax.axis_index("frame")
    partners = [(ds, dc) for ds in range(S) for dc in range(C) if ds or dc]
    others = [(i, ds, dc) for i, (ds, dc) in enumerate(partners) if ds]

    def at(ds, dc):
        return lax.rem(s + ds, S), lax.rem(c + dc, C)

    def columns(group, h):
        return pl.ds(pl.multiple_of((group * heads + h) * HD, HD), HD)

    def token_rows(base, piece):
        return pl.ds(pl.multiple_of(base + piece * tl, tl), tl)

    barrier = pltpu.get_barrier_semaphore()
    for ds, dc in partners:
        s2, c2 = at(ds, dc)
        pl.semaphore_signal(
            barrier, inc=1, device_id={"seq": s2, "cfg": c2}, device_id_type=MESH
        )
    for step in (-1, 1):
        @pl.when((f + step >= 0) & (f + step < F))
        def _():
            for dc in range(C):
                pl.semaphore_signal(
                    barrier, inc=1,
                    device_id={"frame": f + step, "cfg": lax.rem(c + dc, C)},
                    device_id_type=MESH,
                )
    beside = jnp.where(f > 0, C, 0) + jnp.where(f < F - 1, C, 0)
    pl.semaphore_wait(barrier, len(partners) + beside)

    def send_kv(i, ds, dc, h):
        s2, c2 = at(ds, dc)
        return pltpu.make_async_remote_copy(
            src_ref=x_ref.at[pl.ds(1, 2), :, columns(s2 * C + c2, h)],
            dst_ref=kv.at[h, c, :, token_rows(rows, s), :],
            send_sem=a2a_send.at[0, h, i],
            recv_sem=kv_sem.at[h, s, c],
            device_id={"seq": s2, "cfg": c2}, device_id_type=MESH,
        )

    def send_q(i, ds, dc, h):
        s2, c2 = at(ds, dc)
        return pltpu.make_async_remote_copy(
            src_ref=x_ref.at[0, :, columns(s2 * C + c2, h)],
            dst_ref=qb.at[h, c, token_rows(0, s), :],
            send_sem=a2a_send.at[1, h, i],
            recv_sem=q_sem.at[h, s, c],
            device_id={"seq": s2, "cfg": c2}, device_id_type=MESH,
        )

    def own_kv(h):
        return pltpu.make_async_copy(
            x_ref.at[pl.ds(1, 2), :, columns(s * C + c, h)],
            kv.at[h, c, :, token_rows(rows, s), :],
            kv_sem.at[h, s, c],
        )

    def own_q(h):
        return pltpu.make_async_copy(
            x_ref.at[0, :, columns(s * C + c, h)],
            qb.at[h, c, token_rows(0, s), :],
            q_sem.at[h, s, c],
        )

    def halo_base(side):
        return 0 if side == 0 else 2 * rows

    def send_halo(side, dc, h):
        c2 = lax.rem(c + dc, C)
        return pltpu.make_async_remote_copy(
            src_ref=x_ref.at[pl.ds(1, 2), :, columns(s * C + c2, h)],
            dst_ref=kv.at[h, c, :, token_rows(halo_base(side), s), :],
            send_sem=own_send.at[side, h, dc],
            recv_sem=halo_sem.at[side, h, s, c],
            device_id={"frame": f + (1 if side == 0 else -1), "cfg": c2}, device_id_type=MESH,
        )

    def relay(side, i, ds, dc, h):
        s2, b = at(ds, dc)
        return pltpu.make_async_remote_copy(
            src_ref=kv.at[h, b, :, token_rows(rows, s2), :],
            dst_ref=kv.at[h, b, :, token_rows(halo_base(side), s2), :],
            send_sem=relay_send.at[side, h, i],
            recv_sem=halo_sem.at[side, h, s2, b],
            device_id={"frame": f + (1 if side == 0 else -1)}, device_id_type=MESH,
        )

    def send_out(ds, h):
        s2 = lax.rem(s + ds, S)
        return pltpu.make_async_remote_copy(
            src_ref=gb.at[h, token_rows(0, s2), :],
            dst_ref=out_ref.at[h, :, pl.ds(pl.multiple_of(s * HD, HD), HD)],
            send_sem=out_send.at[h, ds - 1],
            recv_sem=out_sem.at[h, s],
            device_id={"seq": s2}, device_id_type=MESH,
        )

    def recv(ref, sem):
        pltpu.make_async_remote_copy(
            src_ref=ref, dst_ref=ref, send_sem=sem, recv_sem=sem,
            device_id={"seq": s}, device_id_type=MESH,
        ).wait_recv()

    up_ok = f < F - 1
    down_ok = f > 0

    @pl.loop(0, heads)
    def _(h):
        for i, (ds, dc) in enumerate(partners):
            send_kv(i, ds, dc, h).start()
        for side, ok in ((0, up_ok), (1, down_ok)):
            @pl.when(ok)
            def _():
                for dc in range(C):
                    send_halo(side, dc, h).start()
        own_kv(h).start()

    @pl.loop(0, heads)
    def _(h):
        for i, (ds, dc) in enumerate(partners):
            send_q(i, ds, dc, h).start()
        own_q(h).start()

    for edge, base in ((f == 0, 0), (f == F - 1, 2 * rows)):
        @pl.when(edge)
        def _():
            @pl.loop(0, heads)
            def _(h):
                kv[h, :, :, pl.ds(base, rows), :] = jnp.zeros((C, 2, rows, HD), kv.dtype)

    @pl.loop(0, heads)
    def _(h):
        for i, ds, dc in others:
            s2, b = at(ds, dc)
            recv(kv.at[h, b, :, token_rows(rows, s2), :], kv_sem.at[h, s2, b])
            for side, ok in ((0, up_ok), (1, down_ok)):
                @pl.when(ok)
                def _():
                    relay(side, i, ds, dc, h).start()

    now = jnp.full((1, HD), time_ref[0], jnp.int32).astype(jnp.float32)
    strength = 1.0 + 4.0 * now / 999.0
    factor = LOG2E / math.sqrt(HD)

    @pl.loop(0, heads)
    def _(h):
        own_kv(h).wait()
        own_q(h).wait()
        for ds, dc in partners:
            s2, b = at(ds, dc)
            if not ds:
                recv(kv.at[h, b, :, token_rows(rows, s2), :], kv_sem.at[h, s2, b])
            recv(qb.at[h, b, token_rows(0, s2), :], q_sem.at[h, s2, b])
        for side, ok in ((0, down_ok), (1, up_ok)):
            @pl.when(ok)
            def _():
                for ds in range(S):
                    for dc in range(C):
                        s2, b = at(ds, dc)
                        recv(
                            kv.at[h, b, :, token_rows(halo_base(side), s2), :],
                            halo_sem.at[side, h, s2, b],
                        )
        window = win_ref[(s * C + c) * heads + h]
        for number in range(frames_here):
            here = f * frames_here + number
            own_shot = seg_ref[here]
            pieces = []
            for offset in range(-W_MAX, W_MAX + 1):
                there = here + offset
                shot = seg_ref[jnp.clip(there, 0, frames - 1)]
                allowed = (
                    (there >= 0) & (there < frames) & (shot == own_shot) & (abs(offset) <= window)
                )
                pieces.append(jnp.full((1, per_frame), jnp.where(allowed, 0.0, NEG), jnp.float32))
            bias = jnp.concatenate(pieces, axis=1)
            start = (frames_here + number - W_MAX) * per_frame
            mixed = []
            for b in range(C):
                query = qb[h, b, pl.ds(number * per_frame, per_frame), :]
                keys = kv[h, b, 0, pl.ds(start, span), :]
                values = kv[h, b, 1, pl.ds(start, span), :]
                scores = lax.dot_general(
                    query, keys, (((1,), (1,)), ((), ())), preferred_element_type=jnp.float32
                ) + bias
                top = jnp.max(scores, axis=1, keepdims=True)
                expd = jnp.exp2((scores - top) * factor)
                total = jnp.sum(expd, axis=1, keepdims=True)
                part = jnp.dot(
                    expd.astype(jnp.bfloat16), values, preferred_element_type=jnp.float32
                )
                mixed.append((part / total).astype(jnp.bfloat16).astype(jnp.float32))
            cond, uncond = mixed
            gb[h, pl.ds(number * per_frame, per_frame), :] = (
                uncond + strength * (cond - uncond)
            ).astype(jnp.bfloat16)
        for ds in range(1, S):
            send_out(ds, h).start()
        out_ref[h, :, pl.ds(pl.multiple_of(s * HD, HD), HD)] = gb[h, token_rows(0, s), :]

    @pl.loop(0, heads)
    def _(h):
        for i, (ds, dc) in enumerate(partners):
            send_kv(i, ds, dc, h).wait_send()
            send_q(i, ds, dc, h).wait_send()
        for side, ok in ((0, up_ok), (1, down_ok)):
            @pl.when(ok)
            def _():
                for dc in range(C):
                    send_halo(side, dc, h).wait_send()
                for i, ds, dc in others:
                    relay(side, i, ds, dc, h).wait_send()
        for ds in range(1, S):
            s2 = lax.rem(s + ds, S)
            send_out(ds, h).wait_send()
            recv(out_ref.at[h, :, pl.ds(pl.multiple_of(s2 * HD, HD), HD)], out_sem.at[h, s2])


def body(qkv, timestep, windows, segments):
    S, C, F = (lax.axis_size(axis) for axis in ("seq", "cfg", "frame"))
    x = jnp.transpose(qkv[0], (1, 0, 2))
    tl = x.shape[1]
    heads = x.shape[2] // HD // (S * C)
    frames_here = segments.shape[0] // F
    assert frames_here >= W_MAX and frames_here == W_MAX
    rows = S * tl
    n = S * C - 1
    dma = pltpu.SemaphoreType.DMA
    out = pl.pallas_call(
        functools.partial(kernel, (S, C, F, heads, tl, frames_here)),
        out_shape=jax.ShapeDtypeStruct((heads, tl, S * HD), jnp.bfloat16),
        in_specs=[pl.BlockSpec(memory_space=pl.ANY)]
        + [pl.BlockSpec(memory_space=pltpu.SMEM)] * 3,
        out_specs=pl.BlockSpec(memory_space=pltpu.VMEM),
        scratch_shapes=[
            pltpu.VMEM((heads, C, 2, 3 * rows, HD), jnp.bfloat16),
            pltpu.VMEM((heads, C, rows, HD), jnp.bfloat16),
            pltpu.VMEM((heads, rows, HD), jnp.bfloat16),
            dma((heads, S, C)),
            dma((heads, S, C)),
            dma((2, heads, S, C)),
            dma((heads, S)),
            dma((2, heads, n)),
            dma((2, heads, C)),
            dma((2, heads, n)),
            dma((heads, max(S - 1, 1))),
        ],
        compiler_params=pltpu.CompilerParams(
            collective_id=0, has_side_effects=True, vmem_limit_bytes=48 * 2**20
        ),
        name="guided_attention",
    )(x, timestep, windows, segments)
    return jnp.transpose(out, (1, 0, 2))


def solution(mesh):
    return jax.shard_map(
        body,
        mesh=mesh,
        in_specs=(P("cfg", ("groups", "frame", "seq"), None, None), P("groups"), P(), P("groups")),
        out_specs=P(("groups", "frame", "seq"), "cfg", None),
        check_vma=False,
    )
```

```python
import functools
import math

import jax
import jax.numpy as jnp
from jax import lax
from jax.experimental import pallas as pl
from jax.experimental.pallas import tpu as pltpu
from jax.sharding import PartitionSpec as P

HD = 128
W_MAX = 2
NEG = -1e30
LOG2E = 1.4426950408889634
MESH = pl.DeviceIdType.MESH


def gather_kernel(heads_all, levels, x_ref, win_ref, out_ref, sem):
    def copy(head, slot):
        return pltpu.make_async_copy(
            x_ref.at[:, :, pl.ds(pl.multiple_of(head * HD, HD), HD)], out_ref.at[slot], sem
        )

    def place(level):
        def step(head, slot):
            hit = win_ref[head] == level

            @pl.when(hit)
            def _():
                copy(head, slot).start()

            return slot + hit.astype(jnp.int32)

        return step

    slot = jnp.int32(0)
    for level in range(levels, -1, -1):
        slot = lax.fori_loop(0, heads_all, place(level), slot)
    pltpu.make_async_copy(out_ref, out_ref, sem).wait()


def kernel(
    dims, x_ref, time_ref, win_ref, seg_ref, out_ref,
    kv, qb, gb, lb, every, rank_ref,
    kv_sem, q_sem, halo_sem, out_sem, a2a_send, own_send, relay_send, out_send, core_send,
    l_sem, l_send,
):
    S, C, F, heads, tl, frames_here, wide, near = dims
    groups = S * C
    rows = S * tl
    per_frame = rows // frames_here
    frames = F * frames_here
    s = lax.axis_index("seq")
    c = lax.axis_index("cfg")
    f = lax.axis_index("frame")
    partners = [(ds, dc) for ds in range(S) for dc in range(C) if ds or dc]
    others = [(i, ds, dc) for i, (ds, dc) in enumerate(partners) if ds]
    up_ok = f < F - 1
    down_ok = f > 0

    def at(ds, dc):
        return lax.rem(s + ds, S), lax.rem(c + dc, C)

    def rank(h, s2, c2):
        return h * groups + s2 * C + c2

    def token_rows(base, piece):
        return pl.ds(pl.multiple_of(base + piece * tl, tl), tl)

    barrier = pltpu.get_barrier_semaphore()
    for ds, dc in partners:
        s2, c2 = at(ds, dc)
        pl.semaphore_signal(
            barrier, inc=1, device_id={"seq": s2, "cfg": c2}, device_id_type=MESH
        )
    for step in (-1, 1):
        @pl.when((f + step >= 0) & (f + step < F))
        def _():
            for dc in range(C):
                pl.semaphore_signal(
                    barrier, inc=1,
                    device_id={"frame": f + step, "cfg": lax.rem(c + dc, C)},
                    device_id_type=MESH,
                )
    beside = jnp.where(f > 0, C, 0) + jnp.where(f < F - 1, C, 0)
    pl.semaphore_wait(barrier, len(partners) + beside)

    def send_kv(i, ds, dc, h):
        s2, c2 = at(ds, dc)
        return pltpu.make_async_remote_copy(
            src_ref=x_ref.at[rank(h, s2, c2), pl.ds(1, 2)],
            dst_ref=kv.at[h, c, :, token_rows(rows, s), :],
            send_sem=a2a_send.at[0, h, i],
            recv_sem=kv_sem.at[h, s, c],
            device_id={"seq": s2, "cfg": c2}, device_id_type=MESH,
        )

    def send_q(i, ds, dc, h):
        s2, c2 = at(ds, dc)
        return pltpu.make_async_remote_copy(
            src_ref=x_ref.at[rank(h, s2, c2), 0],
            dst_ref=qb.at[h, c, token_rows(0, s), :],
            send_sem=a2a_send.at[1, h, i],
            recv_sem=q_sem.at[h, s, c],
            device_id={"seq": s2, "cfg": c2}, device_id_type=MESH,
        )

    def own_kv(h):
        return pltpu.make_async_copy(
            x_ref.at[rank(h, s, c), pl.ds(1, 2)],
            kv.at[h, c, :, token_rows(rows, s), :],
            kv_sem.at[h, s, c],
        )

    def own_q(h):
        return pltpu.make_async_copy(
            x_ref.at[rank(h, s, c), 0], qb.at[h, c, token_rows(0, s), :], q_sem.at[h, s, c]
        )

    def halo_base(side):
        return 0 if side == 0 else 2 * rows

    def neighbour(side):
        return f + (1 if side == 0 else -1)

    def send_halo(side, dc, h):
        c2 = lax.rem(c + dc, C)
        return pltpu.make_async_remote_copy(
            src_ref=x_ref.at[rank(h, s, c2), pl.ds(1, 2)],
            dst_ref=kv.at[h, c, :, token_rows(halo_base(side), s), :],
            send_sem=own_send.at[side, h, dc],
            recv_sem=halo_sem.at[side, h, s, c],
            device_id={"frame": neighbour(side), "cfg": c2}, device_id_type=MESH,
        )

    def relay(side, i, ds, dc, h):
        s2, b = at(ds, dc)
        return pltpu.make_async_remote_copy(
            src_ref=kv.at[h, b, :, token_rows(rows, s2), :],
            dst_ref=kv.at[h, b, :, token_rows(halo_base(side), s2), :],
            send_sem=relay_send.at[side, h, i],
            recv_sem=halo_sem.at[side, h, s2, b],
            device_id={"frame": neighbour(side)}, device_id_type=MESH,
        )

    def crosses(side, s2, reach):
        if reach == W_MAX:
            return s2 >= 0
        return s2 == (S - 1 if side == 0 else 0)

    def send_out(ds, h):
        s2 = lax.rem(s + ds, S)
        return pltpu.make_async_remote_copy(
            src_ref=gb.at[h, token_rows(0, s2), :],
            dst_ref=every.at[rank(h, s, c)],
            send_sem=out_send.at[h, ds - 1],
            recv_sem=out_sem.at[rank(h, s, c)],
            device_id={"seq": s2}, device_id_type=MESH,
        )

    def send_core(h, s2, dc, src):
        return pltpu.make_async_remote_copy(
            src_ref=src,
            dst_ref=every.at[rank(h, s2, c)],
            send_sem=core_send.at[h, s2, dc - 1],
            recv_sem=out_sem.at[rank(h, s2, c)],
            device_id={"cfg": lax.rem(c + dc, C)}, device_id_type=MESH,
        )

    def send_local(h, s2, dc):
        c2 = lax.rem(c + dc, C)
        return pltpu.make_async_remote_copy(
            src_ref=x_ref.at[rank(h, s2, c2)],
            dst_ref=lb.at[h - near, s2, c],
            send_sem=l_send.at[h - near, s2, dc],
            recv_sem=l_sem.at[h - near, s2, c],
            device_id={"cfg": c2}, device_id_type=MESH,
        )

    def own_local(h, s2):
        return pltpu.make_async_copy(
            x_ref.at[rank(h, s2, c)], lb.at[h - near, s2, c], l_sem.at[h - near, s2, c]
        )

    def recv(ref, sem):
        pltpu.make_async_remote_copy(
            src_ref=ref, dst_ref=ref, send_sem=sem, recv_sem=sem,
            device_id={"seq": s}, device_id_type=MESH,
        ).wait_recv()

    phases = ((0, wide, W_MAX), (wide, near, 1))
    sides = ((0, up_ok), (1, down_ok))

    for lo, hi, reach in phases:
        @pl.loop(lo, hi)
        def _(h):
            for i, (ds, dc) in enumerate(partners):
                send_kv(i, ds, dc, h).start()
            for side, ok in sides:
                @pl.when(ok & crosses(side, s, reach))
                def _():
                    for dc in range(C):
                        send_halo(side, dc, h).start()
            own_kv(h).start()

    @pl.loop(near, heads)
    def _(h):
        for s2 in range(S):
            for dc in range(1, C):
                send_local(h, s2, dc).start()
            own_local(h, s2).start()

    @pl.loop(0, near)
    def _(h):
        for i, (ds, dc) in enumerate(partners):
            send_q(i, ds, dc, h).start()
        own_q(h).start()

    for edge, base in ((f == 0, 0), (f == F - 1, 2 * rows)):
        @pl.when(edge)
        def _():
            @pl.loop(0, near)
            def _(h):
                kv[h, :, :, pl.ds(base, rows), :] = jnp.zeros((C, 2, rows, HD), kv.dtype)

    many = [jnp.int32(0)] * (W_MAX + 1)
    for head in range(heads * groups):
        for level in range(W_MAX + 1):
            many[level] = many[level] + jnp.where(win_ref[head] >= level, 1, 0)
    place = [many[level + 1] if level < W_MAX else jnp.int32(0) for level in range(W_MAX + 1)]
    for head in range(heads * groups):
        mine = place[0]
        for level in range(1, W_MAX + 1):
            mine = jnp.where(win_ref[head] == level, place[level], mine)
        rank_ref[head] = mine
        for level in range(W_MAX + 1):
            place[level] = place[level] + jnp.where(win_ref[head] == level, 1, 0)

    now = jnp.full((1, HD), time_ref[0], jnp.int32).astype(jnp.float32)
    strength = 1.0 + 4.0 * now / 999.0
    factor = LOG2E / math.sqrt(HD)

    def attend(query, keys, values, bias):
        scores = lax.dot_general(
            query, keys, (((1,), (1,)), ((), ())), preferred_element_type=jnp.float32
        )
        if bias is not None:
            scores = scores + bias
        top = jnp.max(scores, axis=1, keepdims=True)
        expd = jnp.exp2((scores - top) * factor)
        total = jnp.sum(expd, axis=1, keepdims=True)
        part = jnp.dot(expd.astype(jnp.bfloat16), values, preferred_element_type=jnp.float32)
        return (part / total).astype(jnp.bfloat16).astype(jnp.float32)

    def guide(cond, uncond):
        return (uncond + strength * (cond - uncond)).astype(jnp.bfloat16)

    @pl.loop(near, heads)
    def _(h):
        for s2 in range(S):
            own_local(h, s2).wait()
            for dc in range(1, C):
                b = lax.rem(c + dc, C)
                recv(lb.at[h - near, s2, b], l_sem.at[h - near, s2, b])
            cond, uncond = [
                attend(lb[h - near, s2, b, 0], lb[h - near, s2, b, 1], lb[h - near, s2, b, 2], None)
                for b in range(C)
            ]
            every[rank(h, s2, c)] = guide(cond, uncond)
            for dc in range(1, C):
                send_core(h, s2, dc, every.at[rank(h, s2, c)]).start()

    for lo, hi, reach in phases:
        @pl.loop(lo, hi)
        def _(h):
            for i, ds, dc in others:
                s2, b = at(ds, dc)
                recv(kv.at[h, b, :, token_rows(rows, s2), :], kv_sem.at[h, s2, b])
                for side, ok in sides:
                    @pl.when(ok & crosses(side, s2, reach))
                    def _():
                        relay(side, i, ds, dc, h).start()

    def hand_on(h):
        for ds in range(1, S):
            s2 = lax.rem(s + ds, S)
            ref = every.at[rank(h, s2, c)]
            recv(ref, out_sem.at[rank(h, s2, c)])
            for dc in range(1, C):
                send_core(h, s2, dc, ref).start()

    for lo, hi, reach in phases:
        @pl.loop(lo, hi)
        def _(h):
            own_kv(h).wait()
            own_q(h).wait()
            for ds, dc in partners:
                s2, b = at(ds, dc)
                if not ds:
                    recv(kv.at[h, b, :, token_rows(rows, s2), :], kv_sem.at[h, s2, b])
                recv(qb.at[h, b, token_rows(0, s2), :], q_sem.at[h, s2, b])
            for side, ok in ((0, down_ok), (1, up_ok)):
                for ds in range(S):
                    s2 = lax.rem(s + ds, S)

                    @pl.when(ok & crosses(side, s2, reach))
                    def _():
                        for b in range(C):
                            recv(
                                kv.at[h, b, :, token_rows(halo_base(side), s2), :],
                                halo_sem.at[side, h, s2, b],
                            )
            me = rank(h, s, c)
            window = jnp.int32(0)
            for level in range(1, W_MAX + 1):
                window = window + jnp.where(me < many[level], 1, 0)
            for number in range(frames_here):
                here = f * frames_here + number
                own_shot = seg_ref[here]
                pieces = []
                for offset in range(-reach, reach + 1):
                    there = here + offset
                    shot = seg_ref[jnp.clip(there, 0, frames - 1)]
                    allowed = (
                        (there >= 0) & (there < frames)
                        & (shot == own_shot) & (abs(offset) <= window)
                    )
                    pieces.append(
                        jnp.full((1, per_frame), jnp.where(allowed, 0.0, NEG), jnp.float32)
                    )
                bias = jnp.concatenate(pieces, axis=1)
                keys = pl.ds((frames_here + number - reach) * per_frame, len(pieces) * per_frame)
                mine = pl.ds(number * per_frame, per_frame)
                cond, uncond = [
                    attend(qb[h, b, mine, :], kv[h, b, 0, keys, :], kv[h, b, 1, keys, :], bias)
                    for b in range(C)
                ]
                gb[h, mine, :] = guide(cond, uncond)
            for ds in range(1, S):
                send_out(ds, h).start()
            for dc in range(1, C):
                send_core(h, s, dc, gb.at[h, token_rows(0, s), :]).start()
            every[me] = gb[h, token_rows(0, s), :]

            @pl.when(h > 0)
            def _():
                hand_on(h - 1)

    hand_on(near - 1)

    @pl.loop(0, heads)
    def _(h):
        for s2 in range(S):
            for dc in range(1, C):
                r = rank(h, s2, lax.rem(c + dc, C))
                recv(every.at[r], out_sem.at[r])

    half = heads
    for s2 in range(S):
        for i in range(half):
            head = s2 * (C * half) + c * half + i
            out_ref[i, :, s2 * HD : (s2 + 1) * HD] = every[rank_ref[head]]

    for lo, hi, reach in phases:
        @pl.loop(lo, hi)
        def _(h):
            for i, (ds, dc) in enumerate(partners):
                send_kv(i, ds, dc, h).wait_send()
                send_q(i, ds, dc, h).wait_send()
            for side, ok in sides:
                @pl.when(ok & crosses(side, s, reach))
                def _():
                    for dc in range(C):
                        send_halo(side, dc, h).wait_send()
                for i, ds, dc in others:
                    s2, b = at(ds, dc)

                    @pl.when(ok & crosses(side, s2, reach))
                    def _():
                        relay(side, i, ds, dc, h).wait_send()
            for ds in range(1, S):
                send_out(ds, h).wait_send()

    @pl.loop(0, heads)
    def _(h):
        for s2 in range(S):
            for dc in range(1, C):
                send_core(h, s2, dc, every.at[rank(h, s2, c)]).wait_send()

    @pl.loop(near, heads)
    def _(h):
        for s2 in range(S):
            for dc in range(1, C):
                send_local(h, s2, dc).wait_send()


def body(qkv, timestep, windows, segments):
    S, C, F = (lax.axis_size(axis) for axis in ("seq", "cfg", "frame"))
    x = jnp.transpose(qkv[0], (1, 0, 2))
    tl = x.shape[1]
    heads = x.shape[2] // HD // (S * C)
    frames_here = segments.shape[0] // F
    assert frames_here == W_MAX and heads * S * C * HD == x.shape[2]
    rows = S * tl
    groups = S * C
    n = groups - 1
    dma = pltpu.SemaphoreType.DMA
    ordered = pl.pallas_call(
        functools.partial(gather_kernel, heads * groups, W_MAX),
        out_shape=jax.ShapeDtypeStruct((heads * groups, 3, tl, HD), x.dtype),
        in_specs=[pl.BlockSpec(memory_space=pl.ANY), pl.BlockSpec(memory_space=pltpu.SMEM)],
        out_specs=pl.BlockSpec(memory_space=pltpu.VMEM),
        scratch_shapes=[dma],
        name="order_heads",
        compiler_params=pltpu.CompilerParams(vmem_limit_bytes=56 * 2**20),
    )(x, windows)

    def run(wide, near, number):
        kept = max(heads - near, 1)

        def call(ordered, timestep, windows, segments):
            return pl.pallas_call(
                functools.partial(kernel, (S, C, F, heads, tl, frames_here, wide, near)),
                out_shape=jax.ShapeDtypeStruct((heads, tl, S * HD), jnp.bfloat16),
                in_specs=[pl.BlockSpec(memory_space=pl.ANY)]
                + [pl.BlockSpec(memory_space=pltpu.SMEM)] * 3,
                out_specs=pl.BlockSpec(memory_space=pltpu.VMEM),
                scratch_shapes=[
                    pltpu.VMEM((near, C, 2, 3 * rows, HD), jnp.bfloat16),
                    pltpu.VMEM((near, C, rows, HD), jnp.bfloat16),
                    pltpu.VMEM((near, rows, HD), jnp.bfloat16),
                    pltpu.VMEM((kept, S, C, 3, tl, HD), jnp.bfloat16),
                    pltpu.VMEM((heads * groups, tl, HD), jnp.bfloat16),
                    pltpu.SMEM((heads * groups,), jnp.int32),
                    dma((near, S, C)),
                    dma((near, S, C)),
                    dma((2, near, S, C)),
                    dma((heads * groups,)),
                    dma((2, near, n)),
                    dma((2, near, C)),
                    dma((2, near, n)),
                    dma((near, max(S - 1, 1))),
                    dma((heads, S, C - 1)),
                    dma((kept, S, C)),
                    dma((kept, S, C)),
                ],
                compiler_params=pltpu.CompilerParams(
                    collective_id=number, has_side_effects=True, vmem_limit_bytes=40 * 2**20
                ),
                name=f"guided_attention_{number}",
            )(ordered, timestep, windows, segments)

        return call

    operands = (ordered, timestep, windows, segments)
    wide, near = 3 * heads // 8, 3 * heads // 4
    if wide and tl * frames_here == rows:
        fits = (jnp.sum(windows > 1) <= wide * groups) & (jnp.sum(windows > 0) <= near * groups)
        out = lax.cond(fits, run(wide, near, 1), run(heads, heads, 0), *operands)
    else:
        out = run(heads, heads, 0)(*operands)
    return jnp.transpose(out, (1, 0, 2))


def solution(mesh):
    return jax.shard_map(
        body,
        mesh=mesh,
        in_specs=(P("cfg", ("groups", "frame", "seq"), None, None), P("groups"), P(), P("groups")),
        out_specs=P(("groups", "frame", "seq"), "cfg", None),
        check_vma=False,
    )
```

```python
import functools
import math

import jax
import jax.numpy as jnp
from jax import lax
from jax.experimental import pallas as pl
from jax.experimental.pallas import tpu as pltpu
from jax.sharding import PartitionSpec as P

HD = 128
W_MAX = 2
NEG = -1e30
LOG2E = 1.4426950408889634
MESH = pl.DeviceIdType.MESH


def gather_kernel(heads_all, levels, room, x_ref, win_ref, out_ref, fits_ref, sem):
    def copy(head, slot):
        return pltpu.make_async_copy(
            x_ref.at[:, :, pl.ds(pl.multiple_of(head * HD, HD), HD)], out_ref.at[slot], sem
        )

    def place(level):
        def step(head, slot):
            hit = win_ref[head] == level

            @pl.when(hit)
            def _():
                copy(head, slot).start()

            return slot + hit.astype(jnp.int32)

        return step

    slot = jnp.int32(0)
    fits = jnp.int32(1)
    for level in range(levels, -1, -1):
        slot = lax.fori_loop(0, heads_all, place(level), slot)
        if level:
            fits = fits * (slot <= room[level - 1]).astype(jnp.int32)
    fits_ref[0] = fits
    pltpu.make_async_copy(out_ref, out_ref, sem).wait()


def kernel(
    dims, x_ref, time_ref, win_ref, seg_ref, out_ref,
    kv, qb, gb, lb, every, rank_ref,
    kv_sem, q_sem, halo_sem, out_sem, a2a_send, own_send, relay_send, out_send, core_send,
    l_sem, l_send,
):
    S, C, F, heads, tl, frames_here, wide, near = dims
    groups = S * C
    rows = S * tl
    per_frame = rows // frames_here
    frames = F * frames_here
    s = lax.axis_index("seq")
    c = lax.axis_index("cfg")
    f = lax.axis_index("frame")
    partners = [(ds, dc) for ds in range(S) for dc in range(C) if ds or dc]
    others = [(i, ds, dc) for i, (ds, dc) in enumerate(partners) if ds]
    up_ok = f < F - 1
    down_ok = f > 0

    def at(ds, dc):
        return lax.rem(s + ds, S), lax.rem(c + dc, C)

    def rank(h, s2, c2):
        return h * groups + s2 * C + c2

    def token_rows(base, piece):
        return pl.ds(pl.multiple_of(base + piece * tl, tl), tl)

    barrier = pltpu.get_barrier_semaphore()
    for ds, dc in partners:
        s2, c2 = at(ds, dc)
        pl.semaphore_signal(
            barrier, inc=1, device_id={"seq": s2, "cfg": c2}, device_id_type=MESH
        )
    for step in (-1, 1):
        @pl.when((f + step >= 0) & (f + step < F))
        def _():
            for dc in range(C):
                pl.semaphore_signal(
                    barrier, inc=1,
                    device_id={"frame": f + step, "cfg": lax.rem(c + dc, C)},
                    device_id_type=MESH,
                )
    beside = jnp.where(f > 0, C, 0) + jnp.where(f < F - 1, C, 0)
    pl.semaphore_wait(barrier, len(partners) + beside)

    def send_kv(i, ds, dc, h):
        s2, c2 = at(ds, dc)
        return pltpu.make_async_remote_copy(
            src_ref=x_ref.at[rank(h, s2, c2), pl.ds(1, 2)],
            dst_ref=kv.at[h, c, :, token_rows(rows, s), :],
            send_sem=a2a_send.at[0, h, i],
            recv_sem=kv_sem.at[h, s, c],
            device_id={"seq": s2, "cfg": c2}, device_id_type=MESH,
        )

    def send_q(i, ds, dc, h):
        s2, c2 = at(ds, dc)
        return pltpu.make_async_remote_copy(
            src_ref=x_ref.at[rank(h, s2, c2), 0],
            dst_ref=qb.at[h, c, token_rows(0, s), :],
            send_sem=a2a_send.at[1, h, i],
            recv_sem=q_sem.at[h, s, c],
            device_id={"seq": s2, "cfg": c2}, device_id_type=MESH,
        )

    def own_kv(h):
        return pltpu.make_async_copy(
            x_ref.at[rank(h, s, c), pl.ds(1, 2)],
            kv.at[h, c, :, token_rows(rows, s), :],
            kv_sem.at[h, s, c],
        )

    def own_q(h):
        return pltpu.make_async_copy(
            x_ref.at[rank(h, s, c), 0], qb.at[h, c, token_rows(0, s), :], q_sem.at[h, s, c]
        )

    def halo_base(side):
        return 0 if side == 0 else 2 * rows

    def neighbour(side):
        return f + (1 if side == 0 else -1)

    def send_halo(side, dc, h):
        c2 = lax.rem(c + dc, C)
        return pltpu.make_async_remote_copy(
            src_ref=x_ref.at[rank(h, s, c2), pl.ds(1, 2)],
            dst_ref=kv.at[h, c, :, token_rows(halo_base(side), s), :],
            send_sem=own_send.at[side, h, dc],
            recv_sem=halo_sem.at[side, h, s, c],
            device_id={"frame": neighbour(side), "cfg": c2}, device_id_type=MESH,
        )

    def relay(side, i, ds, dc, h):
        s2, b = at(ds, dc)
        return pltpu.make_async_remote_copy(
            src_ref=kv.at[h, b, :, token_rows(rows, s2), :],
            dst_ref=kv.at[h, b, :, token_rows(halo_base(side), s2), :],
            send_sem=relay_send.at[side, h, i],
            recv_sem=halo_sem.at[side, h, s2, b],
            device_id={"frame": neighbour(side)}, device_id_type=MESH,
        )

    def crosses(side, s2, reach):
        if reach == W_MAX:
            return s2 >= 0
        return s2 == (S - 1 if side == 0 else 0)

    def send_out(ds, h):
        s2 = lax.rem(s + ds, S)
        return pltpu.make_async_remote_copy(
            src_ref=gb.at[h, token_rows(0, s2), :],
            dst_ref=every.at[rank(h, s, c)],
            send_sem=out_send.at[h, ds - 1],
            recv_sem=out_sem.at[rank(h, s, c)],
            device_id={"seq": s2}, device_id_type=MESH,
        )

    def send_core(h, s2, dc, src):
        return pltpu.make_async_remote_copy(
            src_ref=src,
            dst_ref=every.at[rank(h, s2, c)],
            send_sem=core_send.at[h, s2, dc - 1],
            recv_sem=out_sem.at[rank(h, s2, c)],
            device_id={"cfg": lax.rem(c + dc, C)}, device_id_type=MESH,
        )

    def send_local(h, s2, dc):
        c2 = lax.rem(c + dc, C)
        return pltpu.make_async_remote_copy(
            src_ref=x_ref.at[rank(h, s2, c2)],
            dst_ref=lb.at[h - near, s2, c],
            send_sem=l_send.at[h - near, s2, dc],
            recv_sem=l_sem.at[h - near, s2, c],
            device_id={"cfg": c2}, device_id_type=MESH,
        )

    def own_local(h, s2):
        return pltpu.make_async_copy(
            x_ref.at[rank(h, s2, c)], lb.at[h - near, s2, c], l_sem.at[h - near, s2, c]
        )

    def recv(ref, sem):
        pltpu.make_async_remote_copy(
            src_ref=ref, dst_ref=ref, send_sem=sem, recv_sem=sem,
            device_id={"seq": s}, device_id_type=MESH,
        ).wait_recv()

    phases = ((0, wide, W_MAX), (wide, near, 1))
    sides = ((0, up_ok), (1, down_ok))

    for lo, hi, reach in phases:
        @pl.loop(lo, hi)
        def _(h):
            for i, (ds, dc) in enumerate(partners):
                send_kv(i, ds, dc, h).start()
            for side, ok in sides:
                @pl.when(ok & crosses(side, s, reach))
                def _():
                    for dc in range(C):
                        send_halo(side, dc, h).start()
            own_kv(h).start()

    @pl.loop(near, heads)
    def _(h):
        for s2 in range(S):
            for dc in range(1, C):
                send_local(h, s2, dc).start()
            own_local(h, s2).start()

    @pl.loop(0, near)
    def _(h):
        for i, (ds, dc) in enumerate(partners):
            send_q(i, ds, dc, h).start()
        own_q(h).start()

    for edge, base in ((f == 0, 0), (f == F - 1, 2 * rows)):
        @pl.when(edge)
        def _():
            @pl.loop(0, near)
            def _(h):
                kv[h, :, :, pl.ds(base, rows), :] = jnp.zeros((C, 2, rows, HD), kv.dtype)

    many = [jnp.int32(0)] * (W_MAX + 1)
    for head in range(heads * groups):
        for level in range(W_MAX + 1):
            many[level] = many[level] + jnp.where(win_ref[head] >= level, 1, 0)
    place = [many[level + 1] if level < W_MAX else jnp.int32(0) for level in range(W_MAX + 1)]
    for head in range(heads * groups):
        mine = place[0]
        for level in range(1, W_MAX + 1):
            mine = jnp.where(win_ref[head] == level, place[level], mine)
        rank_ref[head] = mine
        for level in range(W_MAX + 1):
            place[level] = place[level] + jnp.where(win_ref[head] == level, 1, 0)

    now = jnp.full((1, HD), time_ref[0], jnp.int32).astype(jnp.float32)
    strength = 1.0 + 4.0 * now / 999.0
    factor = LOG2E / math.sqrt(HD)

    def attend(query, keys, values, bias):
        scores = lax.dot_general(
            query, keys, (((1,), (1,)), ((), ())), preferred_element_type=jnp.float32
        )
        if bias is not None:
            scores = scores + bias
        top = jnp.max(scores, axis=1, keepdims=True)
        expd = jnp.exp2((scores - top) * factor)
        total = jnp.sum(expd, axis=1, keepdims=True)
        part = jnp.dot(expd.astype(jnp.bfloat16), values, preferred_element_type=jnp.float32)
        return (part / total).astype(jnp.bfloat16).astype(jnp.float32)

    def guide(cond, uncond):
        return (uncond + strength * (cond - uncond)).astype(jnp.bfloat16)

    @pl.loop(near, heads)
    def _(h):
        for s2 in range(S):
            own_local(h, s2).wait()
            for dc in range(1, C):
                b = lax.rem(c + dc, C)
                recv(lb.at[h - near, s2, b], l_sem.at[h - near, s2, b])
            cond, uncond = [
                attend(lb[h - near, s2, b, 0], lb[h - near, s2, b, 1], lb[h - near, s2, b, 2], None)
                for b in range(C)
            ]
            every[rank(h, s2, c)] = guide(cond, uncond)
            for dc in range(1, C):
                send_core(h, s2, dc, every.at[rank(h, s2, c)]).start()

    for lo, hi, reach in phases:
        @pl.loop(lo, hi)
        def _(h):
            for i, ds, dc in others:
                s2, b = at(ds, dc)
                recv(kv.at[h, b, :, token_rows(rows, s2), :], kv_sem.at[h, s2, b])
                for side, ok in sides:
                    @pl.when(ok & crosses(side, s2, reach))
                    def _():
                        relay(side, i, ds, dc, h).start()

    def hand_on(h):
        for ds in range(1, S):
            s2 = lax.rem(s + ds, S)
            ref = every.at[rank(h, s2, c)]
            recv(ref, out_sem.at[rank(h, s2, c)])
            for dc in range(1, C):
                send_core(h, s2, dc, ref).start()

    for lo, hi, reach in phases:
        @pl.loop(lo, hi)
        def _(h):
            own_kv(h).wait()
            own_q(h).wait()
            for ds, dc in partners:
                s2, b = at(ds, dc)
                if not ds:
                    recv(kv.at[h, b, :, token_rows(rows, s2), :], kv_sem.at[h, s2, b])
                recv(qb.at[h, b, token_rows(0, s2), :], q_sem.at[h, s2, b])
            for side, ok in ((0, down_ok), (1, up_ok)):
                for ds in range(S):
                    s2 = lax.rem(s + ds, S)

                    @pl.when(ok & crosses(side, s2, reach))
                    def _():
                        for b in range(C):
                            recv(
                                kv.at[h, b, :, token_rows(halo_base(side), s2), :],
                                halo_sem.at[side, h, s2, b],
                            )
            me = rank(h, s, c)
            window = jnp.int32(0)
            for level in range(1, W_MAX + 1):
                window = window + jnp.where(me < many[level], 1, 0)
            for number in range(frames_here):
                here = f * frames_here + number
                own_shot = seg_ref[here]
                pieces = []
                for offset in range(-reach, reach + 1):
                    there = here + offset
                    shot = seg_ref[jnp.clip(there, 0, frames - 1)]
                    allowed = (
                        (there >= 0) & (there < frames)
                        & (shot == own_shot) & (abs(offset) <= window)
                    )
                    pieces.append(
                        jnp.full((1, per_frame), jnp.where(allowed, 0.0, NEG), jnp.float32)
                    )
                bias = jnp.concatenate(pieces, axis=1)
                keys = pl.ds((frames_here + number - reach) * per_frame, len(pieces) * per_frame)
                mine = pl.ds(number * per_frame, per_frame)
                cond, uncond = [
                    attend(qb[h, b, mine, :], kv[h, b, 0, keys, :], kv[h, b, 1, keys, :], bias)
                    for b in range(C)
                ]
                gb[h, mine, :] = guide(cond, uncond)
            for ds in range(1, S):
                send_out(ds, h).start()
            for dc in range(1, C):
                send_core(h, s, dc, gb.at[h, token_rows(0, s), :]).start()
            every[me] = gb[h, token_rows(0, s), :]

            @pl.when(h > 0)
            def _():
                hand_on(h - 1)

            for i, (ds, dc) in enumerate(partners):
                send_kv(i, ds, dc, h).wait_send()
                send_q(i, ds, dc, h).wait_send()
            for side, ok in sides:
                @pl.when(ok & crosses(side, s, reach))
                def _():
                    for dc in range(C):
                        send_halo(side, dc, h).wait_send()
                for i, ds, dc in others:
                    s2, b = at(ds, dc)

                    @pl.when(ok & crosses(side, s2, reach))
                    def _():
                        relay(side, i, ds, dc, h).wait_send()

    @pl.loop(near, heads)
    def _(h):
        for s2 in range(S):
            for dc in range(1, C):
                send_local(h, s2, dc).wait_send()

    hand_on(near - 1)

    @pl.loop(0, heads)
    def _(h):
        for s2 in range(S):
            for dc in range(1, C):
                r = rank(h, s2, lax.rem(c + dc, C))
                recv(every.at[r], out_sem.at[r])

    half = heads
    for s2 in range(S):
        for i in range(half):
            head = s2 * (C * half) + c * half + i
            out_ref[i, :, s2 * HD : (s2 + 1) * HD] = every[rank_ref[head]]

    @pl.loop(0, near)
    def _(h):
        for ds in range(1, S):
            send_out(ds, h).wait_send()

    @pl.loop(0, heads)
    def _(h):
        for s2 in range(S):
            for dc in range(1, C):
                send_core(h, s2, dc, every.at[rank(h, s2, c)]).wait_send()

def body(qkv, timestep, windows, segments):
    S, C, F = (lax.axis_size(axis) for axis in ("seq", "cfg", "frame"))
    x = jnp.transpose(qkv[0], (1, 0, 2))
    tl = x.shape[1]
    heads = x.shape[2] // HD // (S * C)
    frames_here = segments.shape[0] // F
    assert frames_here == W_MAX and heads * S * C * HD == x.shape[2]
    rows = S * tl
    groups = S * C
    n = groups - 1
    dma = pltpu.SemaphoreType.DMA
    wide, near = 3 * heads // 8, 3 * heads // 4
    room = (near * groups,) * (W_MAX - 1) + (wide * groups,)
    ordered, fits = pl.pallas_call(
        functools.partial(gather_kernel, heads * groups, W_MAX, room),
        out_shape=(
            jax.ShapeDtypeStruct((heads * groups, 3, tl, HD), x.dtype),
            jax.ShapeDtypeStruct((1,), jnp.int32),
        ),
        in_specs=[pl.BlockSpec(memory_space=pl.ANY), pl.BlockSpec(memory_space=pltpu.SMEM)],
        out_specs=(
            pl.BlockSpec(memory_space=pltpu.VMEM),
            pl.BlockSpec(memory_space=pltpu.SMEM),
        ),
        scratch_shapes=[dma],
        name="order_heads",
        compiler_params=pltpu.CompilerParams(vmem_limit_bytes=56 * 2**20),
    )(x, windows)

    def run(wide, near, number):
        kept = max(heads - near, 1)

        def call(ordered, timestep, windows, segments):
            return pl.pallas_call(
                functools.partial(kernel, (S, C, F, heads, tl, frames_here, wide, near)),
                out_shape=jax.ShapeDtypeStruct((heads, tl, S * HD), jnp.bfloat16),
                in_specs=[pl.BlockSpec(memory_space=pl.ANY)]
                + [pl.BlockSpec(memory_space=pltpu.SMEM)] * 3,
                out_specs=pl.BlockSpec(memory_space=pltpu.VMEM),
                scratch_shapes=[
                    pltpu.VMEM((near, C, 2, 3 * rows, HD), jnp.bfloat16),
                    pltpu.VMEM((near, C, rows, HD), jnp.bfloat16),
                    pltpu.VMEM((near, rows, HD), jnp.bfloat16),
                    pltpu.VMEM((kept, S, C, 3, tl, HD), jnp.bfloat16),
                    pltpu.VMEM((heads * groups, tl, HD), jnp.bfloat16),
                    pltpu.SMEM((heads * groups,), jnp.int32),
                    dma((near, S, C)),
                    dma((near, S, C)),
                    dma((2, near, S, C)),
                    dma((heads * groups,)),
                    dma((2, near, n)),
                    dma((2, near, C)),
                    dma((2, near, n)),
                    dma((near, max(S - 1, 1))),
                    dma((heads, S, C - 1)),
                    dma((kept, S, C)),
                    dma((kept, S, C)),
                ],
                compiler_params=pltpu.CompilerParams(
                    collective_id=number, has_side_effects=True, vmem_limit_bytes=40 * 2**20
                ),
                name=f"guided_attention_{number}",
            )(ordered, timestep, windows, segments)

        return call

    operands = (ordered, timestep, windows, segments)
    if wide and tl * frames_here == rows:
        out = lax.cond(fits[0] > 0, run(wide, near, 1), run(heads, heads, 0), *operands)
    else:
        out = run(heads, heads, 0)(*operands)
    return jnp.transpose(out, (1, 0, 2))


def solution(mesh):
    return jax.shard_map(
        body,
        mesh=mesh,
        in_specs=(P("cfg", ("groups", "frame", "seq"), None, None), P("groups"), P(), P("groups")),
        out_specs=P(("groups", "frame", "seq"), "cfg", None),
        check_vma=False,
    )
```

```python
import functools
import math

import jax
import jax.numpy as jnp
from jax import lax
from jax.experimental import pallas as pl
from jax.experimental.pallas import tpu as pltpu
from jax.sharding import PartitionSpec as P

HD = 128
W_MAX = 2
NEG = -1e30
LOG2E = 1.4426950408889634
MESH = pl.DeviceIdType.MESH


def gather_kernel(heads_all, levels, room, x_ref, win_ref, out_ref, fits_ref, sem):
    def copy(head, slot):
        return pltpu.make_async_copy(
            x_ref.at[:, :, pl.ds(pl.multiple_of(head * HD, HD), HD)], out_ref.at[slot], sem
        )

    def place(level):
        def step(head, slot):
            hit = win_ref[head] == level

            @pl.when(hit)
            def _():
                copy(head, slot).start()

            return slot + hit.astype(jnp.int32)

        return step

    slot = jnp.int32(0)
    fits = jnp.int32(1)
    for level in range(levels, -1, -1):
        slot = lax.fori_loop(0, heads_all, place(level), slot)
        if level:
            fits = fits * (slot <= room[level - 1]).astype(jnp.int32)
    fits_ref[0] = fits
    pltpu.make_async_copy(out_ref, out_ref, sem).wait()


def kernel(
    dims, x_ref, time_ref, win_ref, seg_ref, out_ref,
    kv, qb, gb, lb, every, rank_ref,
    kv_sem, q_sem, halo_sem, out_sem, a2a_send, own_send, relay_send, out_send, core_send,
    l_sem, l_send,
):
    S, C, F, heads, tl, frames_here, wide, near, short = dims
    groups = S * C
    rows = S * tl
    per_frame = rows // frames_here
    frames = F * frames_here
    s = lax.axis_index("seq")
    c = lax.axis_index("cfg")
    f = lax.axis_index("frame")
    partners = [(ds, dc) for ds in range(S) for dc in range(C) if ds or dc]
    others = [(i, ds, dc) for i, (ds, dc) in enumerate(partners) if ds]
    up_ok = f < F - 1
    down_ok = f > 0

    def at(ds, dc):
        return lax.rem(s + ds, S), lax.rem(c + dc, C)

    def rank(h, s2, c2):
        return h * groups + c2 * S + s2

    def token_rows(base, piece):
        return pl.ds(pl.multiple_of(base + piece * tl, tl), tl)

    def full(core):
        return wide - jnp.where(core > 0, short, 0)

    def shared(core):
        return near - jnp.where(core > 0, short, 0)

    low = near - short

    barrier = pltpu.get_barrier_semaphore()
    for ds, dc in partners:
        s2, c2 = at(ds, dc)
        pl.semaphore_signal(
            barrier, inc=1, device_id={"seq": s2, "cfg": c2}, device_id_type=MESH
        )
    for step in (-1, 1):
        @pl.when((f + step >= 0) & (f + step < F))
        def _():
            for dc in range(C):
                pl.semaphore_signal(
                    barrier, inc=1,
                    device_id={"frame": f + step, "cfg": lax.rem(c + dc, C)},
                    device_id_type=MESH,
                )
    beside = jnp.where(f > 0, C, 0) + jnp.where(f < F - 1, C, 0)
    pl.semaphore_wait(barrier, len(partners) + beside)

    def send_kv(i, ds, dc, h):
        s2, c2 = at(ds, dc)
        return pltpu.make_async_remote_copy(
            src_ref=x_ref.at[rank(h, s2, c2), pl.ds(1, 2)],
            dst_ref=kv.at[h, c, :, token_rows(rows, s), :],
            send_sem=a2a_send.at[0, h, i],
            recv_sem=kv_sem.at[h, s, c],
            device_id={"seq": s2, "cfg": c2}, device_id_type=MESH,
        )

    def send_q(i, ds, dc, h):
        s2, c2 = at(ds, dc)
        return pltpu.make_async_remote_copy(
            src_ref=x_ref.at[rank(h, s2, c2), 0],
            dst_ref=qb.at[h, c, token_rows(0, s), :],
            send_sem=a2a_send.at[1, h, i],
            recv_sem=q_sem.at[h, s, c],
            device_id={"seq": s2, "cfg": c2}, device_id_type=MESH,
        )

    def own_kv(h):
        return pltpu.make_async_copy(
            x_ref.at[rank(h, s, c), pl.ds(1, 2)],
            kv.at[h, c, :, token_rows(rows, s), :],
            kv_sem.at[h, s, c],
        )

    def own_q(h):
        return pltpu.make_async_copy(
            x_ref.at[rank(h, s, c), 0], qb.at[h, c, token_rows(0, s), :], q_sem.at[h, s, c]
        )

    def halo_base(side):
        return 0 if side == 0 else 2 * rows

    def neighbour(side):
        return f + (1 if side == 0 else -1)

    def send_halo(side, dc, h):
        c2 = lax.rem(c + dc, C)
        return pltpu.make_async_remote_copy(
            src_ref=x_ref.at[rank(h, s, c2), pl.ds(1, 2)],
            dst_ref=kv.at[h, c, :, token_rows(halo_base(side), s), :],
            send_sem=own_send.at[side, h, dc],
            recv_sem=halo_sem.at[side, h, s, c],
            device_id={"frame": neighbour(side), "cfg": c2}, device_id_type=MESH,
        )

    def relay(side, i, ds, dc, h):
        s2, b = at(ds, dc)
        return pltpu.make_async_remote_copy(
            src_ref=kv.at[h, b, :, token_rows(rows, s2), :],
            dst_ref=kv.at[h, b, :, token_rows(halo_base(side), s2), :],
            send_sem=relay_send.at[side, h, i],
            recv_sem=halo_sem.at[side, h, s2, b],
            device_id={"frame": neighbour(side)}, device_id_type=MESH,
        )

    def crosses(side, s2, h, core):
        return (h < full(core)) | (s2 == (S - 1 if side == 0 else 0))

    def send_out(ds, h):
        s2 = lax.rem(s + ds, S)
        return pltpu.make_async_remote_copy(
            src_ref=gb.at[h, token_rows(0, s2), :],
            dst_ref=every.at[rank(h, s, c)],
            send_sem=out_send.at[h, ds - 1],
            recv_sem=out_sem.at[rank(h, s, c)],
            device_id={"seq": s2}, device_id_type=MESH,
        )

    def send_core(h, s2, dc, src):
        return pltpu.make_async_remote_copy(
            src_ref=src,
            dst_ref=every.at[rank(h, s2, c)],
            send_sem=core_send.at[h, s2, dc - 1],
            recv_sem=out_sem.at[rank(h, s2, c)],
            device_id={"cfg": lax.rem(c + dc, C)}, device_id_type=MESH,
        )

    def send_local(h, s2, dc):
        c2 = lax.rem(c + dc, C)
        return pltpu.make_async_remote_copy(
            src_ref=x_ref.at[rank(h, s2, c2)],
            dst_ref=lb.at[h - low, s2, c],
            send_sem=l_send.at[h - low, s2, dc],
            recv_sem=l_sem.at[h - low, s2, c],
            device_id={"cfg": c2}, device_id_type=MESH,
        )

    def own_local(h, s2):
        return pltpu.make_async_copy(
            x_ref.at[rank(h, s2, c)], lb.at[h - low, s2, c], l_sem.at[h - low, s2, c]
        )

    def recv(ref, sem):
        pltpu.make_async_remote_copy(
            src_ref=ref, dst_ref=ref, send_sem=sem, recv_sem=sem,
            device_id={"seq": s}, device_id_type=MESH,
        ).wait_recv()

    sides = ((0, up_ok), (1, down_ok))

    def each_partner(h, act):
        for i, (ds, dc) in enumerate(partners):
            @pl.when(h < shared(lax.rem(c + dc, C)))
            def _():
                act(i, ds, dc, h)

    def each_halo(h, act):
        for side, ok in sides:
            for dc in range(C):
                c2 = lax.rem(c + dc, C)

                @pl.when(ok & (h < shared(c2)) & crosses(side, s, h, c2))
                def _():
                    act(send_halo(side, dc, h))

    def each_relay(i, ds, dc, h, act):
        s2, b = at(ds, dc)
        for side, ok in sides:
            @pl.when(ok & crosses(side, s2, h, c))
            def _():
                act(relay(side, i, ds, dc, h))

    def each_local(act):
        @pl.loop(low, heads)
        def _(h):
            for s2 in range(S):
                for dc in range(1, C):
                    @pl.when(h >= shared(lax.rem(c + dc, C)))
                    def _():
                        act(send_local(h, s2, dc))

    @pl.loop(0, near)
    def _(h):
        each_partner(h, lambda *k: send_kv(*k).start())
        each_halo(h, lambda copy: copy.start())

        @pl.when(h < shared(c))
        def _():
            own_kv(h).start()

    each_local(lambda copy: copy.start())

    @pl.loop(shared(c), heads)
    def _(h):
        for s2 in range(S):
            own_local(h, s2).start()

    @pl.loop(0, near)
    def _(h):
        each_partner(h, lambda *k: send_q(*k).start())

        @pl.when(h < shared(c))
        def _():
            own_q(h).start()

    for edge, base in ((f == 0, 0), (f == F - 1, 2 * rows)):
        @pl.when(edge)
        def _():
            @pl.loop(0, near)
            def _(h):
                kv[h, :, :, pl.ds(base, rows), :] = jnp.zeros((C, 2, rows, HD), kv.dtype)

    many = [jnp.int32(0)] * (W_MAX + 1)
    for head in range(heads * groups):
        for level in range(W_MAX + 1):
            many[level] = many[level] + jnp.where(win_ref[head] >= level, 1, 0)
    place = [many[level + 1] if level < W_MAX else jnp.int32(0) for level in range(W_MAX + 1)]
    for head in range(heads * groups):
        mine = place[0]
        for level in range(1, W_MAX + 1):
            mine = jnp.where(win_ref[head] == level, place[level], mine)
        rank_ref[head] = mine
        for level in range(W_MAX + 1):
            place[level] = place[level] + jnp.where(win_ref[head] == level, 1, 0)

    now = jnp.full((1, HD), time_ref[0], jnp.int32).astype(jnp.float32)
    strength = 1.0 + 4.0 * now / 999.0
    factor = LOG2E / math.sqrt(HD)

    def attend(query, keys, values, bias):
        scores = lax.dot_general(
            query, keys, (((1,), (1,)), ((), ())), preferred_element_type=jnp.float32
        )
        if bias is not None:
            scores = scores + bias
        top = jnp.max(scores, axis=1, keepdims=True)
        expd = jnp.exp2((scores - top) * factor)
        total = jnp.sum(expd, axis=1, keepdims=True)
        part = jnp.dot(expd.astype(jnp.bfloat16), values, preferred_element_type=jnp.float32)
        return (part / total).astype(jnp.bfloat16).astype(jnp.float32)

    def guide(cond, uncond):
        return (uncond + strength * (cond - uncond)).astype(jnp.bfloat16)

    @pl.loop(shared(c), heads)
    def _(h):
        for s2 in range(S):
            own_local(h, s2).wait()
            for dc in range(1, C):
                b = lax.rem(c + dc, C)
                recv(lb.at[h - low, s2, b], l_sem.at[h - low, s2, b])
            cond, uncond = [
                attend(lb[h - low, s2, b, 0], lb[h - low, s2, b, 1], lb[h - low, s2, b, 2], None)
                for b in range(C)
            ]
            every[rank(h, s2, c)] = guide(cond, uncond)
            for dc in range(1, C):
                send_core(h, s2, dc, every.at[rank(h, s2, c)]).start()

    @pl.loop(0, shared(c))
    def _(h):
        for i, ds, dc in others:
            s2, b = at(ds, dc)
            recv(kv.at[h, b, :, token_rows(rows, s2), :], kv_sem.at[h, s2, b])
            each_relay(i, ds, dc, h, lambda copy: copy.start())

    def hand_on(h):
        for ds in range(1, S):
            s2 = lax.rem(s + ds, S)
            ref = every.at[rank(h, s2, c)]
            recv(ref, out_sem.at[rank(h, s2, c)])
            for dc in range(1, C):
                send_core(h, s2, dc, ref).start()

    for lo, hi, reach in ((0, full(c), W_MAX), (full(c), shared(c), 1)):
        @pl.loop(lo, hi)
        def _(h):
            own_kv(h).wait()
            own_q(h).wait()
            for ds, dc in partners:
                s2, b = at(ds, dc)
                if not ds:
                    recv(kv.at[h, b, :, token_rows(rows, s2), :], kv_sem.at[h, s2, b])
                recv(qb.at[h, b, token_rows(0, s2), :], q_sem.at[h, s2, b])
            for side, ok in ((0, down_ok), (1, up_ok)):
                for ds in range(S):
                    s2 = lax.rem(s + ds, S)

                    @pl.when(ok & crosses(side, s2, h, c))
                    def _():
                        for b in range(C):
                            recv(
                                kv.at[h, b, :, token_rows(halo_base(side), s2), :],
                                halo_sem.at[side, h, s2, b],
                            )
            me = rank(h, s, c)
            window = jnp.int32(0)
            for level in range(1, W_MAX + 1):
                window = window + jnp.where(me < many[level], 1, 0)
            for number in range(frames_here):
                here = f * frames_here + number
                own_shot = seg_ref[here]
                pieces = []
                for offset in range(-reach, reach + 1):
                    there = here + offset
                    shot = seg_ref[jnp.clip(there, 0, frames - 1)]
                    allowed = (
                        (there >= 0) & (there < frames)
                        & (shot == own_shot) & (abs(offset) <= window)
                    )
                    pieces.append(
                        jnp.full((1, per_frame), jnp.where(allowed, 0.0, NEG), jnp.float32)
                    )
                bias = jnp.concatenate(pieces, axis=1)
                keys = pl.ds((frames_here + number - reach) * per_frame, len(pieces) * per_frame)
                mine = pl.ds(number * per_frame, per_frame)
                cond, uncond = [
                    attend(qb[h, b, mine, :], kv[h, b, 0, keys, :], kv[h, b, 1, keys, :], bias)
                    for b in range(C)
                ]
                gb[h, mine, :] = guide(cond, uncond)
            for ds in range(1, S):
                send_out(ds, h).start()
            for dc in range(1, C):
                send_core(h, s, dc, gb.at[h, token_rows(0, s), :]).start()
            every[me] = gb[h, token_rows(0, s), :]

            @pl.when(h > 0)
            def _():
                hand_on(h - 1)

    hand_on(shared(c) - 1)

    @pl.loop(0, near)
    def _(h):
        each_partner(h, lambda *k: send_kv(*k).wait_send())
        each_partner(h, lambda *k: send_q(*k).wait_send())
        each_halo(h, lambda copy: copy.wait_send())

    @pl.loop(0, shared(c))
    def _(h):
        for i, ds, dc in others:
            each_relay(i, ds, dc, h, lambda copy: copy.wait_send())

    each_local(lambda copy: copy.wait_send())

    @pl.loop(0, heads)
    def _(h):
        for s2 in range(S):
            for dc in range(1, C):
                r = rank(h, s2, lax.rem(c + dc, C))
                recv(every.at[r], out_sem.at[r])

    half = heads
    for s2 in range(S):
        for i in range(half):
            head = s2 * (C * half) + c * half + i
            out_ref[i, :, s2 * HD : (s2 + 1) * HD] = every[rank_ref[head]]

    @pl.loop(0, shared(c))
    def _(h):
        for ds in range(1, S):
            send_out(ds, h).wait_send()

    @pl.loop(0, heads)
    def _(h):
        for s2 in range(S):
            for dc in range(1, C):
                send_core(h, s2, dc, every.at[rank(h, s2, c)]).wait_send()

def body(qkv, timestep, windows, segments):
    S, C, F = (lax.axis_size(axis) for axis in ("seq", "cfg", "frame"))
    x = jnp.transpose(qkv[0], (1, 0, 2))
    tl = x.shape[1]
    heads = x.shape[2] // HD // (S * C)
    frames_here = segments.shape[0] // F
    assert frames_here == W_MAX and heads * S * C * HD == x.shape[2]
    rows = S * tl
    groups = S * C
    n = groups - 1
    dma = pltpu.SemaphoreType.DMA
    wide, near = 3 * heads // 8, 3 * heads // 4
    short = 1 if heads > 4 else 0
    cut = short * S * (C - 1)
    room = (near * groups - cut,) * (W_MAX - 1) + (wide * groups - cut,)
    ordered, fits = pl.pallas_call(
        functools.partial(gather_kernel, heads * groups, W_MAX, room),
        out_shape=(
            jax.ShapeDtypeStruct((heads * groups, 3, tl, HD), x.dtype),
            jax.ShapeDtypeStruct((1,), jnp.int32),
        ),
        in_specs=[pl.BlockSpec(memory_space=pl.ANY), pl.BlockSpec(memory_space=pltpu.SMEM)],
        out_specs=(
            pl.BlockSpec(memory_space=pltpu.VMEM),
            pl.BlockSpec(memory_space=pltpu.SMEM),
        ),
        scratch_shapes=[dma],
        name="order_heads",
        compiler_params=pltpu.CompilerParams(vmem_limit_bytes=56 * 2**20),
    )(x, windows)

    def run(wide, near, short, number):
        kept = max(heads - near + short, 1)

        def call(ordered, timestep, windows, segments):
            return pl.pallas_call(
                functools.partial(kernel, (S, C, F, heads, tl, frames_here, wide, near, short)),
                out_shape=jax.ShapeDtypeStruct((heads, tl, S * HD), jnp.bfloat16),
                in_specs=[pl.BlockSpec(memory_space=pl.ANY)]
                + [pl.BlockSpec(memory_space=pltpu.SMEM)] * 3,
                out_specs=pl.BlockSpec(memory_space=pltpu.VMEM),
                scratch_shapes=[
                    pltpu.VMEM((near, C, 2, 3 * rows, HD), jnp.bfloat16),
                    pltpu.VMEM((near, C, rows, HD), jnp.bfloat16),
                    pltpu.VMEM((near, rows, HD), jnp.bfloat16),
                    pltpu.VMEM((kept, S, C, 3, tl, HD), jnp.bfloat16),
                    pltpu.VMEM((heads * groups, tl, HD), jnp.bfloat16),
                    pltpu.SMEM((heads * groups,), jnp.int32),
                    dma((near, S, C)),
                    dma((near, S, C)),
                    dma((2, near, S, C)),
                    dma((heads * groups,)),
                    dma((2, near, n)),
                    dma((2, near, C)),
                    dma((2, near, n)),
                    dma((near, max(S - 1, 1))),
                    dma((heads, S, C - 1)),
                    dma((kept, S, C)),
                    dma((kept, S, C)),
                ],
                compiler_params=pltpu.CompilerParams(
                    collective_id=number, has_side_effects=True, vmem_limit_bytes=40 * 2**20
                ),
                name=f"guided_attention_{number}",
            )(ordered, timestep, windows, segments)

        return call

    operands = (ordered, timestep, windows, segments)
    if wide and tl * frames_here == rows:
        out = lax.cond(fits[0] > 0, run(wide, near, short, 1), run(heads, heads, 0, 0), *operands)
    else:
        out = run(heads, heads, 0, 0)(*operands)
    return jnp.transpose(out, (1, 0, 2))


def solution(mesh):
    return jax.shard_map(
        body,
        mesh=mesh,
        in_specs=(P("cfg", ("groups", "frame", "seq"), None, None), P("groups"), P(), P("groups")),
        out_specs=P(("groups", "frame", "seq"), "cfg", None),
        check_vma=False,
    )
```
